32 devices in a mesh: group: 4 (over x, core), fsdp: 8 (over z, y).
Axes of the slice: x: 2, y: 2, z: 4, core: 2. Of those that a mesh axis runs over, the one named last changes fastest.
Arguments:
- resid_in: bfloat16 [64, 320, 1536], P(('group', 'fsdp')), may hold values from -44 to 44
- attn_out: bfloat16 [64, 320, 1536], P(('group', 'fsdp')), may hold values from -6 to 6
- target_rows: bfloat16 [64, 320, 1536], P(('group', 'fsdp')), may hold values from -6 to 6
- out_weight: bfloat16 [1536, 1536], P('fsdp'), may hold values from -0.15625 to 0.15625
- norm_gain: bfloat16 [1536], replicated, may hold values from 0.099609375 to 1.8984375
- seq_lengths: int32 [64], replicated, may hold values from 33 to 320, as said below
- prompt_ids: int32 [64], replicated, may hold values from 0 to 31, as said below
- log_offsets: float32 [64], replicated, may hold values from -48 to 57
- plan_dest: int32 [64, 5], replicated, may hold values from -1 to 3, as said below
- plan_slot: int32 [64, 5], replicated, may hold values from -1 to 5, as said below
Outputs:
- resid_grad: bfloat16 [64, 320, 1536], P(('group', 'fsdp'))
- attn_grad: bfloat16 [64, 320, 1536], P(('group', 'fsdp'))
- weight_grad: float32 [1536, 1536], P('fsdp')
- loss: float32 [], replicated
The draws below stay inside these ranges and needn't reach their ends.
Inputs may be any that keep to these rules, and one draw needn't show every extreme that they name: `seq_lengths`: A sequence of length l covers its first ceil(l / 64) buckets; the sequences of one index of fsdp cover exactly 24 buckets together, and on every index of fsdp some device has all 2 sequences of length 320. `plan_dest`: -1 exactly for buckets that the sequence doesn't cover. Among the devices of one index of fsdp, each works on exactly 6 buckets, and no device sends more than 3 of its buckets to one device; some device sends exactly 3 to one device. `plan_slot`: -1 where plan_dest is -1. For one index of fsdp, every pair of working device and position below 6 is taken by exactly one bucket. `prompt_ids`: the sequences of index g along group (g * 2 * 8 onwards) belong to prompts g * 8 to g * 8 + 7, each prompt with exactly 2 sequences.
All inputs are finite; a program needn't handle non-finite values.
Results may differ from the reference program's by a relative error of at most 0.005.
Values may be sent and summed in bfloat16 or wider, within the bound.
No kernel may reach another device: no remote copies, remote signals or barrier semaphores. Data moves between devices by JAX's collectives and lax.ppermute only.
A program may use at most 128 MiB of HBM per device.

```python
import math
import jax
import jax.numpy as jnp
from jax import lax

D = 1536
SEQ_DEV = 2
NBLK = 5
BLOCK = 64
PPG = 8
LMAX = 320
SEQS = 64
PROMPTS = 32
SAMPLES = 2
N_GROUP = 4
N_FSDP = 8


def block_plan(key):
    base = jax.random.fold_in(key, 101)
    count = N_GROUP * SEQ_DEV
    pos = jnp.arange(count, dtype=jnp.int32)
    device = pos // SEQ_DEV
    rotate = jax.random.randint(jax.random.fold_in(base, 1), (N_FSDP, 1), 0, N_GROUP)
    relative = (device[None, :] - rotate) % N_GROUP
    forced = relative == 0
    blocks = jnp.where(forced, NBLK, jnp.where((relative == 1) | (relative == 2), 2, 3)).astype(jnp.int32)

    def move(step, blocks):
        step_key = jax.random.fold_in(jax.random.fold_in(base, 2), step)
        pair = jax.random.randint(step_key, (2, N_FSDP, 1), 0, count)
        source = pos[None, :] == pair[0]
        target = pos[None, :] == pair[1]
        source_blocks = jnp.sum(jnp.where(source, blocks, 0), axis=1, keepdims=True)
        target_blocks = jnp.sum(jnp.where(target, blocks, 0), axis=1, keepdims=True)
        source_forced = jnp.any(source & forced, axis=1, keepdims=True)
        target_forced = jnp.any(target & forced, axis=1, keepdims=True)
        accept = ~source_forced & ~target_forced & (pair[0] != pair[1]) & (source_blocks > 1) & (target_blocks < NBLK)
        accept_int = accept.astype(jnp.int32)
        return blocks - accept_int * source.astype(jnp.int32) + accept_int * target.astype(jnp.int32)
    blocks = lax.fori_loop(0, 8 * count, move, blocks)
    trimmed = jax.random.randint(jax.random.fold_in(base, 3), (N_FSDP, count), 0, BLOCK // 2)
    trimmed = jnp.where(forced, 0, trimmed)
    lengths = (blocks * BLOCK - trimmed).astype(jnp.int32)
    covered = (jnp.arange(NBLK, dtype=jnp.int32)[None, None, :] < blocks[:, :, None]).reshape(N_FSDP, count * NBLK)
    order = jnp.cumsum(covered.astype(jnp.int32), axis=1) - 1
    dest = jnp.where(covered, order % N_GROUP, -1).astype(jnp.int32)
    slot = jnp.where(covered, order // N_GROUP, -1).astype(jnp.int32)
    lengths = jnp.transpose(lengths.reshape(N_FSDP, N_GROUP, SEQ_DEV), (1, 0, 2)).reshape(-1)
    dest = jnp.transpose(dest.reshape(N_FSDP, N_GROUP, SEQ_DEV, NBLK), (1, 0, 2, 3)).reshape(-1, NBLK)
    slot = jnp.transpose(slot.reshape(N_FSDP, N_GROUP, SEQ_DEV, NBLK), (1, 0, 2, 3)).reshape(-1, NBLK)
    return (lengths, dest, slot)


def draw_seq_lengths(key, part):
    return block_plan(key)[0]


def draw_plan_dest(key, part):
    return block_plan(key)[1]


def draw_plan_slot(key, part):
    return block_plan(key)[2]


def draw_prompt_ids(key, part):
    keys = jax.random.split(jax.random.fold_in(key, 202), N_GROUP)

    def shuffle_row(row_key):
        return jax.random.permutation(row_key, SEQ_DEV * N_FSDP)
    shuffled = jax.vmap(shuffle_row)(keys)
    ids = jnp.arange(N_GROUP, dtype=jnp.int32)[:, None] * PPG + shuffled % PPG
    return ids.reshape(-1).astype(jnp.int32)


def draw_log_offsets(key, part):
    seq = jnp.arange(SEQS, dtype=jnp.int32)
    column = (seq // SEQ_DEV % N_FSDP).astype(jnp.float32)
    spread = 4.0 + 8.0 * column / max(N_FSDP - 1, 1)
    inner = jax.random.fold_in(key, 303)
    values = jnp.clip(jax.random.normal(inner, (SEQS,), jnp.float32), -4.0, 4.0) * spread
    return values.astype(jnp.float32)


def draw_resid_in(key, part):
    inner = jax.random.fold_in(key, 404)
    values = jnp.clip(jax.random.normal(inner, (SEQS, LMAX, D), jnp.float32), -6.0, 6.0)
    return values.astype(jnp.bfloat16)


def levels(rng, extent, cuts, least, top_value):
    level, own = 1.0, jax.random.fold_in(rng, 6)
    for axis_at, shards_of in cuts:
        steps = jnp.exp(jax.random.uniform(jax.random.fold_in(own, axis_at), (shards_of,), jnp.float32, least / len(cuts), top_value / len(cuts)))
        level = level * jnp.repeat(steps, extent[axis_at] // shards_of).reshape([-1 if axis == axis_at else 1 for axis in range(len(extent))])
    return level


def noise(stream_key, extent, deviation, bound, shards=(), kind=jnp.bfloat16):
    result = deviation * jax.random.normal(stream_key, extent, jnp.float32)
    if shards:
        result = result * levels(stream_key, extent, shards, -0.22, 0.18)
    return jnp.clip(result, -bound, bound).astype(kind)


def setup_inputs(seed: int = 0) -> dict:
    key_list = jax.random.split(jax.random.key(seed), 11)
    return {
        "resid_in": draw_resid_in(jax.random.fold_in(key_list[10], 71), 0),
        "attn_out": noise(key_list[1], (SEQS, LMAX, D), 1.0, 6.0, ((0, 32),)),
        "target_rows": noise(key_list[2], (SEQS, LMAX, D), 1.0, 6.0, ((0, 32),)),
        "out_weight": noise(key_list[3], (D, D), D ** -0.5, 0.15625, ((0, 8),)),
        "norm_gain": jnp.clip(1.0 + 0.18 * jax.random.normal(key_list[4], (D,), jnp.float32), 0.099609375, 1.8984375).astype(jnp.bfloat16),
        "seq_lengths": draw_seq_lengths(jax.random.fold_in(key_list[10], 71), 0),
        "prompt_ids": draw_prompt_ids(jax.random.fold_in(key_list[10], 71), 0),
        "log_offsets": draw_log_offsets(jax.random.fold_in(key_list[10], 71), 0),
        "plan_dest": draw_plan_dest(jax.random.fold_in(key_list[10], 71), 0),
        "plan_slot": draw_plan_slot(jax.random.fold_in(key_list[10], 71), 0),
    }


EPS = 1e-06

def forward_rows(x_rows, o_rows, e_rows, weight, gain, mask):
    width = x_rows.shape[-1]
    mixed = x_rows.astype(jnp.float32) + jnp.dot(o_rows, weight, preferred_element_type=jnp.float32)
    scale_inv = lax.rsqrt(lax.optimization_barrier(jnp.mean(mixed * mixed, axis=-1, keepdims=True)) + EPS)
    normed = mixed * scale_inv * gain.astype(jnp.float32)
    token_logp = lax.optimization_barrier(jnp.sum(normed * e_rows.astype(jnp.float32), axis=-1)) * mask / math.sqrt(width)
    return (mixed, scale_inv, token_logp)

def backward_rows(mixed, scale_inv, e_rows, gain, coeff, weight):
    width = mixed.shape[-1]
    gained = coeff[:, None] * e_rows.astype(jnp.float32) * gain.astype(jnp.float32) / math.sqrt(width)
    inner = lax.optimization_barrier(jnp.mean(mixed * gained, axis=-1, keepdims=True))
    grad_rows = (scale_inv * gained - mixed * scale_inv ** 3 * inner).astype(jnp.bfloat16)
    attn_rows = lax.dot_general(grad_rows, weight, (((1,), (1,)), ((), ())), preferred_element_type=jnp.float32).astype(jnp.bfloat16)
    return (grad_rows, attn_rows)

def reference(resid_in, attn_out, target_rows, out_weight, norm_gain, seq_lengths, prompt_ids, log_offsets, plan_dest, plan_slot):
    positions = jnp.arange(LMAX, dtype=jnp.int32)
    masks = (positions[None, :] < seq_lengths[:, None]).astype(jnp.float32)

    def seq_forward(items):
        x_rows, o_rows, e_rows, mask = items
        mixed, scale_inv, token_logp = forward_rows(x_rows, o_rows, e_rows, out_weight, norm_gain, mask)
        return jnp.sum(token_logp)
    seq_logp = lax.map(seq_forward, (resid_in, attn_out, target_rows, masks))
    delta = seq_logp + log_offsets
    member = (prompt_ids[:, None] == jnp.arange(PROMPTS, dtype=jnp.int32)[None, :]).astype(jnp.float32)
    baseline = lax.optimization_barrier(jnp.sum(member * delta[:, None], axis=0)) / SAMPLES
    centred = delta - lax.optimization_barrier(jnp.sum(member * baseline[None, :], axis=1))
    loss = jnp.sum(centred * centred) / (SEQS * LMAX)

    def seq_backward(total, items):
        x_rows, o_rows, e_rows, mask, weight_seq = items
        mixed, scale_inv, token_logp = forward_rows(x_rows, o_rows, e_rows, out_weight, norm_gain, mask)
        grad_rows, attn_rows = backward_rows(mixed, scale_inv, e_rows, norm_gain, weight_seq * mask, out_weight)
        total = total + lax.dot_general(o_rows, grad_rows, (((0,), (0,)), ((), ())), preferred_element_type=jnp.float32)
        return (total, (grad_rows, attn_rows))
    start = jnp.zeros((D, D), jnp.float32)
    total, outputs = lax.scan(seq_backward, start, (resid_in, attn_out, target_rows, masks, centred))
    return (outputs[0], outputs[1], total / SEQS, loss)
```

```python
import functools
import math

import jax
import jax.numpy as jnp
import numpy as np
from jax import lax
from jax.experimental import pallas as pl
from jax.experimental.pallas import tpu as pltpu
from jax.sharding import PartitionSpec as P

PPG = 8
EPS = 1e-06
BOTH = ("group", "fsdp")


def ring_order(n):
    y = 1
    while 2 * y * y < n:
        y *= 2
    if 2 * y * y != n or y < 2:
        return list(range(n))
    z = n // y
    cells = [(k, 0) for k in range(z)]
    for turn, k in enumerate(reversed(range(z))):
        row = range(1, y) if turn % 2 == 0 else range(y - 1, 0, -1)
        cells += [(k, j) for j in row]
    return [k * y + j for k, j in cells]


def ring_table(n):
    order = ring_order(n)
    pos = {f: p for p, f in enumerate(order)}
    table = np.zeros((2, n, n), np.int32)
    for c in range(2):
        sign = 1 if c == 0 else -1
        for f in range(n):
            for d in range(n):
                table[c, f, d] = order[(pos[f] + sign * d) % n]
    return table


def copy_shards(n, meta, table, shards, wbuf, sems):
    rows = shards[0].shape[0]
    base = (lax.rem(meta[0], 2) * n + meta[1]) * n
    half = n // 2
    steps = [0] + [n - k for k in range(1, half)] + list(range(1, half)) + [half]
    copies = []
    for at, (d, shard) in enumerate(zip(steps, shards)):
        first = pl.multiple_of(table[base + d] * rows, 16)
        copies.append(pltpu.make_async_copy(shard, wbuf.at[pl.ds(first, rows), :], sems.at[at]))
    for copy in copies:
        copy.start()
    for copy in copies:
        copy.wait()


def forward_kernel(n, seq_dev, lmax, bt, meta, table, lens, offs, o_ref, x_ref, e_ref, gain_ref, *rest):
    shards, (r_ref, pay_ref, wbuf, sums, sems) = rest[:n], rest[n:]
    step = pl.program_id(0)
    blocks = lmax // bt
    width = o_ref.shape[-1]

    @pl.when(step == 0)
    def _():
        copy_shards(n, meta, table, shards, wbuf, sems)
        for s in range(seq_dev):
            sums[s] = 0.0

    first = (meta[0] * n + meta[1]) * seq_dev
    seq = step // blocks
    mixed = x_ref[0].astype(jnp.float32) + jnp.dot(
        o_ref[0], wbuf[...], preferred_element_type=jnp.float32
    )
    scale_inv = lax.rsqrt(jnp.mean(mixed * mixed, axis=-1, keepdims=True) + EPS)
    gained = e_ref[0].astype(jnp.float32) * (gain_ref[...].astype(jnp.float32) / math.sqrt(width))
    inner = jnp.sum(mixed * gained, axis=-1, keepdims=True)
    token = lax.rem(step, blocks) * bt + lax.broadcasted_iota(jnp.int32, (bt, 1), 0)
    covered = token < lens[first + seq]
    logp = jnp.where(covered, inner * scale_inv, 0.0)
    sums[seq] += jnp.sum(logp)
    keep = jnp.where(covered, scale_inv, 0.0)
    pull = scale_inv * scale_inv * (inner / width)
    r_ref[0] = (keep * (gained - mixed * pull)).astype(r_ref.dtype)

    @pl.when(step == pl.num_programs(0) - 1)
    def _():
        lane = lax.broadcasted_iota(jnp.int32, pay_ref.shape, 2)
        pay = jnp.zeros(pay_ref.shape, jnp.float32)
        for s in range(seq_dev):
            pay = jnp.where(lane == s, sums[s] + offs[first + s], pay)
        pay_ref[...] = pay


def contract(coeffs, ot_own, ot_par, r_own, r_par, cols):
    total = None
    seq_dev = ot_own.shape[0]
    for q, c in enumerate(coeffs):
        ot, r, s = (ot_own, r_own, q) if q < seq_dev else (ot_par, r_par, q - seq_dev)
        part = c * jnp.dot(ot[s], r[s, :, cols], preferred_element_type=jnp.float32)
        total = part if total is None else total + part
    return total


def first_kernel(n, seq_dev, samples, meta, table, pids, recv, pidm, ot_own, ot_par, r_own, r_par, out, c_ref):
    me = meta[0] * n + meta[1]
    core = lax.rem(meta[0], 2)
    par = me + (1 - 2 * core) * n
    dm = recv[:, 0, :]
    ids = pidm[...]
    row = lax.broadcasted_iota(jnp.int32, dm.shape, 0)
    lane = lax.broadcasted_iota(jnp.int32, dm.shape, 1)
    coeffs = []
    for q in range(2 * seq_dev):
        dev, s = (me, q) if q < seq_dev else (par, q - seq_dev)
        pid = pids[dev * seq_dev + s]
        own = jnp.where((row == dev) & (lane == s), dm, 0.0)
        same = jnp.where(ids == pid, dm, 0.0)
        coeffs.append(jnp.sum(own, keepdims=True) - jnp.sum(same, keepdims=True) / samples)
    for q, c in enumerate(coeffs):
        c_ref[q : q + 1, :] = jnp.broadcast_to(c, (1, c_ref.shape[1]))
    out[...] = contract(coeffs, ot_own, ot_par, r_own, r_par, slice(None)).astype(out.dtype)


def rest_kernel(n, seq_dev, meta, table, c_ref, ot_own, ot_par, r_own, r_par, out):
    step = pl.program_id(0)
    core = lax.rem(meta[0], 2)
    half = jnp.where(lax.rem(step, 2) == 0, core, 1 - core)
    cols = out.shape[-1]
    take = pl.ds(pl.multiple_of(half * cols, 128), cols)
    coeffs = [c_ref[q : q + 1, 0:1] for q in range(2 * seq_dev)]
    out[0] = contract(coeffs, ot_own, ot_par, r_own, r_par, take).astype(out.dtype)


def attn_kernel(n, blocks, meta, table, c_ref, r_ref, *rest):
    shards, (g_ref, a_ref, wbuf, sems) = rest[:n], rest[n:]
    step = pl.program_id(0)

    @pl.when(step == 0)
    def _():
        copy_shards(n, meta, table, shards, wbuf, sems)

    c = c_ref[pl.ds(step // blocks, 1), 0:1]
    r = r_ref[0]
    g_ref[0] = (c * r.astype(jnp.float32)).astype(g_ref.dtype)
    rows = lax.dot_general(
        r, wbuf[...], (((1,), (1,)), ((), ())), preferred_element_type=jnp.float32
    )
    a_ref[0] = (c * rows).astype(a_ref.dtype)


def local(
    order,
    resid_in,
    attn_out,
    target_rows,
    out_weight,
    norm_gain,
    seq_lengths,
    prompt_ids,
    log_offsets,
    plan_dest,
    plan_slot,
):
    seq_dev, lmax, width = resid_in.shape
    rows = out_weight.shape[0]
    n_group = lax.axis_size("group")
    n = lax.axis_size("fsdp")
    n_dev = n_group * n
    half_n = n // 2
    half_w = width // 2
    total_seqs = seq_lengths.shape[0]
    prompts = PPG * n_group
    samples = seq_dev * n // PPG
    group_idx = lax.axis_index("group")
    fsdp_idx = lax.axis_index("fsdp")
    bt = lmax // 2
    blocks = lmax // bt
    bf16, f32 = jnp.bfloat16, jnp.float32
    any_spec = pl.BlockSpec(memory_space=pl.ANY)

    along = []
    for g in range(n_group):
        sign = 1 if g % 2 == 0 else -1
        for p in range(n):
            along.append((g * n + order[p], g * n + order[(p + sign) % n]))
    pair = [(g, g ^ 1) for g in range(n_group)]

    def ring(value):
        return lax.ppermute(value, BOTH, along)

    def swap(value):
        return lax.ppermute(value, "group", pair)

    behind, ahead = [], []
    piece = out_weight
    for _ in range(half_n - 1):
        piece = ring(piece)
        behind.append(piece)
        ahead.append(swap(piece))
    opposite = ring(piece)
    shards = [out_weight, *behind, *ahead, opposite]

    ot_own = jnp.swapaxes(attn_out, 1, 2)
    ot_par = swap(ot_own)

    meta = jnp.stack([group_idx, fsdp_idx]).astype(jnp.int32)
    table = jnp.asarray(ring_table(n).reshape(-1))
    gain = norm_gain.reshape(1, width)
    pidm = jnp.pad(
        prompt_ids.reshape(n_dev, seq_dev), ((0, 0), (0, 128 - seq_dev)), constant_values=-1
    )

    flops = 2 * seq_dev * lmax * width * width
    token_block = pl.BlockSpec((1, bt, width), lambda i, *_: (i // blocks, i % blocks, 0))
    r_own, pay = pl.pallas_call(
        functools.partial(forward_kernel, n, seq_dev, lmax, bt),
        grid_spec=pltpu.PrefetchScalarGridSpec(
            num_scalar_prefetch=4,
            grid=(seq_dev * blocks,),
            in_specs=[token_block] * 3
            + [pl.BlockSpec((1, width), lambda i, *_: (0, 0))]
            + [any_spec] * n,
            out_specs=[
                token_block,
                pl.BlockSpec((n_dev, 8, 128), lambda i, *_: (0, 0, 0)),
            ],
            scratch_shapes=[
                pltpu.VMEM((width, width), bf16),
                pltpu.SMEM((seq_dev,), f32),
                pltpu.SemaphoreType.DMA((n,)),
            ],
        ),
        out_shape=[
            jax.ShapeDtypeStruct((seq_dev, lmax, width), bf16),
            jax.ShapeDtypeStruct((n_dev, 8, 128), f32),
        ],
        cost_estimate=pl.CostEstimate(
            flops=flops, bytes_accessed=2 * width * (width + 4 * seq_dev * lmax), transcendentals=0
        ),
        name="forward_rows",
    )(meta, table, seq_lengths, log_offsets, attn_out, resid_in, target_rows, gain, *shards)

    r_par = swap(r_own)
    recv = lax.all_to_all(pay, BOTH, 0, 0, tiled=True)

    def row_block(d):
        def index(i, meta, table, *_):
            return (0, table[((meta[0] % 2) * n + meta[1]) * n + d], 0)

        return index

    def rest_rows(i, meta, table, *_):
        return (0, table[((meta[0] % 2) * n + meta[1]) * n + half_n - 1 - i // 2], 0)

    sent, coeff = pl.pallas_call(
        functools.partial(first_kernel, n, seq_dev, samples),
        grid_spec=pltpu.PrefetchScalarGridSpec(
            num_scalar_prefetch=3,
            grid=(1,),
            in_specs=[
                pl.BlockSpec((n_dev, 8, 128), lambda i, *_: (0, 0, 0)),
                pl.BlockSpec((n_dev, 128), lambda i, *_: (0, 0)),
                pl.BlockSpec((seq_dev, rows, lmax), row_block(half_n)),
                pl.BlockSpec((seq_dev, rows, lmax), row_block(half_n)),
                pl.BlockSpec((seq_dev, lmax, half_w), lambda i, meta, *_: (0, 0, meta[0] % 2)),
                pl.BlockSpec((seq_dev, lmax, half_w), lambda i, meta, *_: (0, 0, meta[0] % 2)),
            ],
            out_specs=[
                pl.BlockSpec((rows, half_w), lambda i, *_: (0, 0)),
                pl.BlockSpec((8, 128), lambda i, *_: (0, 0)),
            ],
        ),
        out_shape=[
            jax.ShapeDtypeStruct((rows, half_w), bf16),
            jax.ShapeDtypeStruct((8, 128), f32),
        ],
        cost_estimate=pl.CostEstimate(
            flops=2 * flops // n // 2,
            bytes_accessed=2 * 2 * seq_dev * lmax * (half_w + rows),
            transcendentals=0,
        ),
        name="first_rows",
    )(meta, table, prompt_ids, recv, pidm, ot_own, ot_par, r_own, r_par)

    got = ring(sent)

    parts = pl.pallas_call(
        functools.partial(rest_kernel, n, seq_dev),
        grid_spec=pltpu.PrefetchScalarGridSpec(
            num_scalar_prefetch=2,
            grid=(n - 1,),
            in_specs=[
                pl.BlockSpec((8, 128), lambda i, *_: (0, 0)),
                pl.BlockSpec((seq_dev, rows, lmax), rest_rows),
                pl.BlockSpec((seq_dev, rows, lmax), rest_rows),
                pl.BlockSpec((seq_dev, lmax, width), lambda i, *_: (0, 0, 0)),
                pl.BlockSpec((seq_dev, lmax, width), lambda i, *_: (0, 0, 0)),
            ],
            out_specs=pl.BlockSpec((1, rows, half_w), lambda i, *_: (i, 0, 0)),
        ),
        out_shape=jax.ShapeDtypeStruct((n - 1, rows, half_w), bf16),
        cost_estimate=pl.CostEstimate(
            flops=flops,
            bytes_accessed=2 * 4 * seq_dev * lmax * width + width * width,
            transcendentals=0,
        ),
        name="rest_rows",
    )(meta, table, coeff, ot_own, ot_par, r_own, r_par)

    resid_grad, attn_grad = pl.pallas_call(
        functools.partial(attn_kernel, n, blocks),
        grid_spec=pltpu.PrefetchScalarGridSpec(
            num_scalar_prefetch=2,
            grid=(seq_dev * blocks,),
            in_specs=[pl.BlockSpec((8, 128), lambda i, *_: (0, 0)), token_block] + [any_spec] * n,
            out_specs=[token_block, token_block],
            scratch_shapes=[
                pltpu.VMEM((width, width), bf16),
                pltpu.SemaphoreType.DMA((n,)),
            ],
        ),
        out_shape=[jax.ShapeDtypeStruct((seq_dev, lmax, width), bf16)] * 2,
        cost_estimate=pl.CostEstimate(
            flops=flops, bytes_accessed=2 * width * (width + 3 * seq_dev * lmax), transcendentals=0
        ),
        name="attn_rows",
    )(meta, table, coeff, r_own, *shards)

    def add(a, b):
        return (a.astype(f32) + b.astype(f32)).astype(bf16)

    run = jnp.stack([add(got, parts[0]), parts[1]])
    for k in range(1, half_n):
        run = ring(run)
        if k < half_n - 1:
            run = add(run, parts[2 * k : 2 * k + 2])
    run = run.astype(f32)
    mine = (run[0] + parts[n - 2].astype(f32) + swap(run[1].astype(bf16)).astype(f32)).astype(bf16)
    bit = 2
    while bit < n_group:
        other = lax.ppermute(mine, "group", [(g, g ^ bit) for g in range(n_group)])
        whole = mine.astype(f32) + other.astype(f32)
        mine = whole.astype(bf16)
        bit *= 2
    whole = whole / total_seqs
    other = swap(whole)
    low = lax.rem(group_idx, 2) == 0
    weight_grad = jnp.concatenate(
        [jnp.where(low, whole, other), jnp.where(low, other, whole)], axis=1
    )

    delta = recv[:, 0, :seq_dev].reshape(-1)
    member = (prompt_ids[:, None] == jnp.arange(prompts, dtype=jnp.int32)[None, :]).astype(f32)
    baseline = jnp.sum(member * delta[:, None], axis=0) / samples
    centred = delta - jnp.sum(member * baseline[None, :], axis=1)
    loss = jnp.sum(centred * centred) / (total_seqs * lmax)
    return (resid_grad, attn_grad, weight_grad, loss)


def solution(mesh):
    order = ring_order(mesh.shape["fsdp"])
    return jax.shard_map(
        functools.partial(local, order),
        mesh=mesh,
        in_specs=(
            P(("group", "fsdp"), None, None),
            P(("group", "fsdp"), None, None),
            P(("group", "fsdp"), None, None),
            P("fsdp", None),
            P(),
            P(),
            P(),
            P(),
            P(),
            P(),
        ),
        out_specs=(
            P(("group", "fsdp"), None, None),
            P(("group", "fsdp"), None, None),
            P("fsdp", None),
            P(),
        ),
        check_vma=False,
    )
```
